32 devices in a mesh: replica: 2 (over x), shard: 16 (over z, y, core).
Axes of the slice: x: 2, y: 2, z: 4, core: 2. Of those that a mesh axis runs over, the one named last changes fastest.
Arguments:
- tokens: bfloat16 [32, 197, 768], P(('replica', 'shard')), may hold values from -6 to 6
- cotangent: bfloat16 [32, 197, 768], P(('replica', 'shard')), may hold values from -6 to 6
- norm1_gain: bfloat16 [768], P('shard'), may hold values from 0.5 to 1.5
- norm1_bias: bfloat16 [768], P('shard'), may hold values from -3 to 3
- proj_in: bfloat16 [768, 2304], P('shard'), may hold values from -0.21875 to 0.21875
- query_bias: bfloat16 [768], P('shard'), may hold values from -6 to 6
- value_bias: bfloat16 [768], P('shard'), may hold values from -3 to 3
- proj_out: bfloat16 [768, 768], P('shard'), may hold values from -0.625 to 0.625
- out_bias: bfloat16 [768], P('shard'), may hold values from -3 to 3
- norm2_gain: bfloat16 [768], P('shard'), may hold values from 0.5 to 1.5
- norm2_bias: bfloat16 [768], P('shard'), may hold values from -3 to 3
- router: bfloat16 [768, 16], P('shard'), may hold values from -0.21875 to 0.21875
- up_weight: bfloat16 [16, 768, 3072], P('shard'), may hold values from -0.21875 to 0.21875
- up_bias: bfloat16 [16, 3072], P('shard'), may hold values from -3 to 3
- down_weight: bfloat16 [16, 3072, 768], P('shard'), may hold values from -1.75 to 1.75
- down_bias: bfloat16 [16, 768], P('shard'), may hold values from -24 to 24
- expert_ids: int32 [6304, 2], P(('replica', 'shard')), may hold values from 0 to 15, as said below
- slot_ids: int32 [6304, 2], P(('replica', 'shard')), may hold values from 0 to 24, as said below
Outputs:
- block_out: bfloat16 [32, 197, 768], P(('replica', 'shard'))
- tokens_grad: bfloat16 [32, 197, 768], P(('replica', 'shard'))
- norm1_gain_grad: float32 [768], P('shard')
- norm1_bias_grad: float32 [768], P('shard')
- proj_in_grad: float32 [768, 2304], P('shard')
- query_bias_grad: float32 [768], P('shard')
- value_bias_grad: float32 [768], P('shard')
- proj_out_grad: float32 [768, 768], P('shard')
- out_bias_grad: float32 [768], P('shard')
- norm2_gain_grad: float32 [768], P('shard')
- norm2_bias_grad: float32 [768], P('shard')
- router_grad: float32 [768, 16], P('shard')
- up_weight_grad: float32 [16, 768, 3072], P('shard', None, 'replica')
- up_bias_grad: float32 [16, 3072], P('shard', 'replica')
- down_weight_grad: float32 [16, 3072, 768], P('shard', 'replica')
- down_bias_grad: float32 [16, 768], P('shard', 'replica')
The draws below stay inside these ranges and needn't reach their ends.
Inputs may be any that keep to these rules, and one draw needn't show every extreme that they name: `expert_ids`: each row names two different experts. On every device the first 25 rows all name one expert first, the same expert on every device. `slot_ids`: within the rows of one device, first choices are placed before second choices, each in row order; a pair's slot is the number of that device's earlier pairs naming the same expert, stored as 24 when it is 24 or more, which marks a dropped pair. Kept pairs of one device never share an expert and a slot; on every device one expert has all 24 slots filled and a pair dropped.
All inputs are finite; a program needn't handle non-finite values.
Results may differ from the reference program's by a relative error of at most 0.022.
Values may be sent and summed in bfloat16 or wider, within the bound.
A program may use at most 128 MiB of HBM per device.

```python
import jax
import jax.numpy as jnp
from jax import lax

D = 768
HEADS = 12
HDIM = 64
FF = 3072
SEQ = 197
EXPERTS = 16
TOK_DEV = 197
IMAGES = 32
TOKENS = 6304
CAP = 24
N_REPLICA = 2
N_SHARD = 16


def route_pairs(key):
    base = jax.random.fold_in(key, 101)
    subkeys = jax.random.split(base, 5)
    row_index = jnp.arange(TOKENS, dtype=jnp.int32) % TOK_DEV
    smallest = jnp.minimum(jnp.minimum(jax.random.randint(subkeys[0], (TOKENS,), 0, EXPERTS), jax.random.randint(subkeys[1], (TOKENS,), 0, EXPERTS)), jax.random.randint(subkeys[2], (TOKENS,), 0, EXPERTS))
    ranked = jnp.where(row_index < CAP + 1, 0, smallest).astype(jnp.int32)
    shuffle = jax.random.permutation(subkeys[3], EXPERTS).astype(jnp.int32)
    offset = jax.random.randint(subkeys[4], (TOKENS,), 1, EXPERTS).astype(jnp.int32)
    first_pick = shuffle[ranked]
    second_pick = shuffle[(ranked + offset) % EXPERTS]
    blocks = TOKENS // TOK_DEV
    queued = jnp.concatenate([first_pick.reshape(blocks, TOK_DEV), second_pick.reshape(blocks, TOK_DEV)], axis=1)
    onehot = (queued[:, :, None] == jnp.arange(EXPERTS, dtype=jnp.int32)[None, None, :]).astype(jnp.int32)
    before = jnp.cumsum(onehot, axis=1) - onehot
    placed = jnp.minimum(jnp.sum(before * onehot, axis=2), CAP).astype(jnp.int32)
    slot_first = placed[:, :TOK_DEV].reshape(TOKENS)
    slot_second = placed[:, TOK_DEV:].reshape(TOKENS)
    return (jnp.stack([first_pick, second_pick], axis=1), jnp.stack([slot_first, slot_second], axis=1))


def draw_expert_ids(key, part):
    return route_pairs(key)[0]


def draw_slot_ids(key, part):
    return route_pairs(key)[1]


def level_of(key, extent, shards, low, largest):
    def one(axis_at, parts):
        steps = jax.random.uniform(jax.random.fold_in(jax.random.fold_in(key, 6), axis_at), (parts,), jnp.float32, low / len(shards), largest / len(shards))
        return jnp.repeat(jnp.exp(steps), extent[axis_at] // parts).reshape((-1,) + (1,) * (len(extent) - axis_at - 1))

    level = one(*shards[0])
    for cut in shards[1:]:
        level = level * one(*cut)
    return level


def gaussian(key, extent, scale, limit, cuts=(), kind=jnp.bfloat16):
    entries = scale * jax.random.normal(key, extent, jnp.float32)
    if cuts:
        entries = entries * level_of(key, extent, cuts, -0.22, 0.18)
    return jnp.clip(entries, -limit, limit).astype(kind)


def setup_inputs(seed: int = 0) -> dict:
    seeds = jax.random.split(jax.random.key(seed), 19)
    return {
        "tokens": gaussian(seeds[0], (IMAGES, SEQ, D), 1.0, 6.0, ((0, 32),)),
        "cotangent": gaussian(seeds[1], (IMAGES, SEQ, D), 1.0, 6.0, ((0, 32),)),
        "norm1_gain": jnp.clip(1.0 + 0.1 * jax.random.normal(seeds[2], (D,), jnp.float32), 0.5, 1.5).astype(jnp.bfloat16),
        "norm1_bias": gaussian(seeds[3], (D,), 0.5, 3.0, ((0, 16),)),
        "proj_in": gaussian(seeds[4], (D, 3 * D), D ** -0.5, 0.21875, ((0, 16),)),
        "query_bias": gaussian(seeds[5], (D,), 1.0, 6.0, ((0, 16),)),
        "value_bias": gaussian(seeds[6], (D,), 0.5, 3.0, ((0, 16),)),
        "proj_out": gaussian(seeds[7], (D, D), (D // 8) ** -0.5, 0.625, ((0, 16),)),
        "out_bias": gaussian(seeds[8], (D,), 0.5, 3.0, ((0, 16),)),
        "norm2_gain": jnp.clip(1.0 + 0.1 * jax.random.normal(seeds[9], (D,), jnp.float32), 0.5, 1.5).astype(jnp.bfloat16),
        "norm2_bias": gaussian(seeds[10], (D,), 0.5, 3.0, ((0, 16),)),
        "router": gaussian(seeds[11], (D, EXPERTS), D ** -0.5, 0.21875, ((0, 16),)),
        "up_weight": gaussian(seeds[12], (EXPERTS, D, FF), D ** -0.5, 0.21875, ((0, 16),)),
        "up_bias": gaussian(seeds[13], (EXPERTS, FF), 0.5, 3.0, ((0, 16),)),
        "down_weight": gaussian(seeds[14], (EXPERTS, FF, D), (max(FF // 256, 1)) ** -0.5, 1.75, ((0, 16),)),
        "down_bias": gaussian(seeds[15], (EXPERTS, D), 4.0, 24.0, ((0, 16),)),
        "expert_ids": draw_expert_ids(jax.random.fold_in(seeds[18], 71), 0),
        "slot_ids": draw_slot_ids(jax.random.fold_in(seeds[18], 71), 0),
    }


EPS = 1e-06
SQRT_HALF = 0.7071067811865476
INV_ROOT_TWO_PI = 0.3989422804014327

def layer_norm(rows_in, norm_gain, norm_shift):
    average = lax.optimization_barrier(jnp.mean(rows_in, axis=-1, keepdims=True))
    centred = rows_in - average
    inv_std = lax.rsqrt(lax.optimization_barrier(jnp.mean(centred * centred, axis=-1, keepdims=True)) + EPS)
    normed = centred * inv_std
    return (normed, inv_std, normed * norm_gain + norm_shift)

def norm_back(grad_rows, normed, inv_std, norm_gain):
    scaled = grad_rows * norm_gain
    inner = scaled - lax.optimization_barrier(jnp.mean(scaled, axis=-1, keepdims=True)) - normed * lax.optimization_barrier(jnp.mean(scaled * normed, axis=-1, keepdims=True))
    return (inner * inv_std, lax.optimization_barrier(jnp.sum(grad_rows * normed, axis=0)), lax.optimization_barrier(jnp.sum(grad_rows, axis=0)))

def gelu_parts(pre_act):
    cumul = 0.5 * (1.0 + lax.erf(pre_act * SQRT_HALF))
    return (pre_act * cumul, cumul + pre_act * jnp.exp(-0.5 * pre_act * pre_act) * INV_ROOT_TWO_PI)

def split_heads(flat_rows):
    return flat_rows.reshape(-1, SEQ, HEADS, HDIM).astype(jnp.float32)

def route_table(id_block, slot_block):
    positions = jnp.arange(EXPERTS * CAP, dtype=jnp.int32)
    tables = []
    for choose in range(2):
        kept = slot_block[:, choose] < CAP
        target = jnp.where(kept, id_block[:, choose] * CAP + slot_block[:, choose], -1).astype(jnp.int32)
        tables.append((target[:, None] == positions[None, :]).astype(jnp.bfloat16))
    return tables

def pick_table(id_block):
    labels = jnp.arange(EXPERTS, dtype=jnp.int32)
    return [(id_block[:, choose][:, None] == labels[None, :]).astype(jnp.float32) for choose in range(2)]

def block_pass(dense, expert_set, tok_block, cot_block, id_block, slot_block):
    gain_one, shift_one, proj_full, query_shift, value_shift, outproj_full, out_shift, gain_two, shift_two, router_full = dense
    up_full, up_shift, down_full, down_shift = expert_set
    tok_rows = tok_block.astype(jnp.float32)
    normed_one, inv_one, pre_one = layer_norm(tok_rows, gain_one.astype(jnp.float32), shift_one.astype(jnp.float32))
    act_one = pre_one.astype(jnp.bfloat16)
    mixed = jnp.dot(act_one, proj_full, preferred_element_type=jnp.float32)
    query_part = (mixed[:, :D] + query_shift.astype(jnp.float32)).astype(jnp.bfloat16)
    key_part = mixed[:, D:2 * D].astype(jnp.bfloat16)
    value_part = (mixed[:, 2 * D:] + value_shift.astype(jnp.float32)).astype(jnp.bfloat16)
    query_heads = split_heads(query_part)
    key_heads = split_heads(key_part)
    value_heads = split_heads(value_part)
    scores = jnp.einsum('ishd,ithd->ihst', query_heads, key_heads) * HDIM ** (-0.5)
    log_total = jnp.log(lax.optimization_barrier(jnp.sum(jnp.exp(scores), axis=-1)))
    attn_probs = jnp.exp(scores - log_total[..., None]).astype(jnp.bfloat16)
    context = jnp.einsum('ihst,ithd->ishd', attn_probs.astype(jnp.float32), value_heads).reshape(-1, D).astype(jnp.bfloat16)
    resid = tok_rows + jnp.dot(context, outproj_full, preferred_element_type=jnp.float32) + out_shift.astype(jnp.float32)
    normed_two, inv_two, pre_two = layer_norm(resid, gain_two.astype(jnp.float32), shift_two.astype(jnp.float32))
    hidden = pre_two.astype(jnp.bfloat16)
    logits = jnp.dot(hidden, router_full, preferred_element_type=jnp.float32)
    exp_logits = jnp.exp(logits)
    gate_probs = exp_logits / lax.optimization_barrier(jnp.sum(exp_logits, axis=-1, keepdims=True))
    routes = route_table(id_block, slot_block)
    picks = pick_table(id_block)
    buffer = (jnp.dot(routes[0].T, hidden, preferred_element_type=jnp.float32) + jnp.dot(routes[1].T, hidden, preferred_element_type=jnp.float32)).astype(jnp.bfloat16).reshape(EXPERTS, CAP, D)
    buffer_wide = buffer.astype(jnp.float32)
    expert_pre = jnp.einsum('ecd,edf->ecf', buffer_wide, up_full) + up_shift[:, None, :]
    act_val, slope = gelu_parts(expert_pre)
    active = act_val.astype(jnp.bfloat16)
    active_wide = active.astype(jnp.float32)
    expert_out = (jnp.einsum('ecf,efd->ecd', active_wide, down_full) + down_shift[:, None, :]).astype(jnp.bfloat16).reshape(EXPERTS * CAP, D)
    gathered_pair = [jnp.dot(table, expert_out, preferred_element_type=jnp.float32) for table in routes]
    gate_pair = [lax.optimization_barrier(jnp.sum(gate_probs * pick, axis=-1)) for pick in picks]
    moe_sum = gate_pair[0][:, None] * gathered_pair[0] + gate_pair[1][:, None] * gathered_pair[1]
    out_rows = (resid + moe_sum).astype(jnp.bfloat16)
    grad_out = cot_block.astype(jnp.float32)
    grad_gate = [lax.optimization_barrier(jnp.sum(grad_out * part, axis=-1)) for part in gathered_pair]
    sent = [(gate[:, None] * grad_out).astype(jnp.bfloat16) for gate in gate_pair]
    grad_buffer = (jnp.dot(routes[0].T, sent[0], preferred_element_type=jnp.float32) + jnp.dot(routes[1].T, sent[1], preferred_element_type=jnp.float32)).astype(jnp.bfloat16).reshape(EXPERTS, CAP, D)
    grad_buffer_wide = grad_buffer.astype(jnp.float32)
    grad_active = jnp.einsum('ecd,efd->ecf', grad_buffer_wide, down_full)
    grad_pre = (grad_active * slope).astype(jnp.bfloat16)
    grad_pre_wide = grad_pre.astype(jnp.float32)
    expert_terms = (jnp.einsum('ecd,ecf->edf', buffer_wide, grad_pre_wide), lax.optimization_barrier(jnp.sum(grad_pre_wide, axis=1)), jnp.einsum('ecf,ecd->efd', active_wide, grad_buffer_wide), lax.optimization_barrier(jnp.sum(grad_buffer_wide, axis=1)))
    grad_in = jnp.einsum('ecf,edf->ecd', grad_pre_wide, up_full).astype(jnp.bfloat16).reshape(EXPERTS * CAP, D)
    grad_moe = jnp.dot(routes[0], grad_in, preferred_element_type=jnp.float32) + jnp.dot(routes[1], grad_in, preferred_element_type=jnp.float32)
    grad_gates = picks[0] * grad_gate[0][:, None] + picks[1] * grad_gate[1][:, None]
    grad_logits = (gate_probs * (grad_gates - lax.optimization_barrier(jnp.sum(gate_probs * grad_gates, axis=-1, keepdims=True)))).astype(jnp.bfloat16)
    router_term = jnp.dot(hidden.T, grad_logits, preferred_element_type=jnp.float32)
    grad_norm_two = grad_moe + jnp.dot(grad_logits, router_full.T, preferred_element_type=jnp.float32)
    grad_resid_two, gain_two_term, shift_two_term = norm_back(grad_norm_two, normed_two, inv_two, gain_two.astype(jnp.float32))
    grad_resid = grad_out + grad_resid_two
    resid_bf = grad_resid.astype(jnp.bfloat16)
    out_shift_term = lax.optimization_barrier(jnp.sum(grad_resid, axis=0))
    outproj_term = jnp.dot(context.T, resid_bf, preferred_element_type=jnp.float32)
    grad_context = jnp.dot(resid_bf, outproj_full.T, preferred_element_type=jnp.float32).astype(jnp.bfloat16)
    context_heads = split_heads(grad_context)
    scores_again = jnp.einsum('ishd,ithd->ihst', query_heads, key_heads) * HDIM ** (-0.5)
    probs_full = jnp.exp(scores_again - log_total[..., None])
    grad_probs = jnp.einsum('ishd,ithd->ihst', context_heads, value_heads)
    grad_scores = (probs_full * (grad_probs - lax.optimization_barrier(jnp.sum(probs_full * grad_probs, axis=-1, keepdims=True))) * HDIM ** (-0.5)).astype(jnp.bfloat16).astype(jnp.float32)
    probs_bf = probs_full.astype(jnp.bfloat16).astype(jnp.float32)
    grad_value = jnp.einsum('ihst,ishd->ithd', probs_bf, context_heads).reshape(-1, D)
    grad_query = jnp.einsum('ihst,ithd->ishd', grad_scores, key_heads).reshape(-1, D)
    grad_key = jnp.einsum('ihst,ishd->ithd', grad_scores, query_heads).reshape(-1, D)
    grad_mixed = jnp.concatenate([grad_query, grad_key, grad_value], axis=1).astype(jnp.bfloat16)
    proj_term = jnp.dot(act_one.T, grad_mixed, preferred_element_type=jnp.float32)
    grad_act = jnp.dot(grad_mixed, proj_full.T, preferred_element_type=jnp.float32)
    grad_tok_norm, gain_one_term, shift_one_term = norm_back(grad_act, normed_one, inv_one, gain_one.astype(jnp.float32))
    grad_rows = (grad_resid + grad_tok_norm).astype(jnp.bfloat16)
    dense_terms = (gain_one_term, shift_one_term, proj_term, lax.optimization_barrier(jnp.sum(grad_query, axis=0)), lax.optimization_barrier(jnp.sum(grad_value, axis=0)), outproj_term, out_shift_term, gain_two_term, shift_two_term, router_term)
    return (out_rows, grad_rows, dense_terms, expert_terms)

def add_pairs(first_set, second_set):
    return tuple((left + right for left, right in zip(first_set, second_set)))

def reference(tokens, cotangent, norm1_gain, norm1_bias, proj_in, query_bias, value_bias, proj_out, out_bias, norm2_gain, norm2_bias, router, up_weight, up_bias, down_weight, down_bias, expert_ids, slot_ids):
    dense = (norm1_gain, norm1_bias, proj_in, query_bias, value_bias, proj_out, out_bias, norm2_gain, norm2_bias, router)
    expert_set = (up_weight.astype(jnp.float32), up_bias.astype(jnp.float32), down_weight.astype(jnp.float32), down_bias.astype(jnp.float32))
    grouped = (tokens.reshape(N_REPLICA, N_SHARD, TOK_DEV, D), cotangent.reshape(N_REPLICA, N_SHARD, TOK_DEV, D), expert_ids.reshape(N_REPLICA, N_SHARD, TOK_DEV, 2), slot_ids.reshape(N_REPLICA, N_SHARD, TOK_DEV, 2))
    dense_zero = tuple((jnp.zeros(param.shape, jnp.float32) for param in dense))
    expert_zero = tuple((jnp.zeros(param.shape, jnp.float32) for param in expert_set))

    def shard_step(carry, block):
        dense_acc, expert_acc = carry
        out_rows, grad_rows, dense_terms, expert_terms = block_pass(dense, expert_set, block[0], block[1], block[2], block[3])
        return ((add_pairs(dense_acc, dense_terms), add_pairs(expert_acc, expert_terms)), (out_rows, grad_rows))

    def replica_step(carry, group):
        dense_acc, expert_acc = carry
        (dense_acc, expert_group), out_pair = lax.scan(shard_step, (dense_acc, expert_zero), group)
        rounded = tuple((lax.optimization_barrier(term.astype(jnp.bfloat16)).astype(jnp.float32) for term in expert_group))
        return ((dense_acc, add_pairs(expert_acc, rounded)), out_pair)
    (dense_grads, expert_grads), out_pair = lax.scan(replica_step, (dense_zero, expert_zero), grouped)
    block_out = out_pair[0].reshape(IMAGES, SEQ, D)
    tokens_grad = out_pair[1].reshape(IMAGES, SEQ, D)
    return (block_out, tokens_grad, dense_grads[0], dense_grads[1], dense_grads[2], dense_grads[3], dense_grads[4], dense_grads[5], dense_grads[6], dense_grads[7], dense_grads[8], dense_grads[9], expert_grads[0], expert_grads[1], expert_grads[2], expert_grads[3])
```

```python
import jax
import jax.numpy as jnp
from jax import lax
from jax.sharding import PartitionSpec as P

D = 768
HEADS = 12
HDIM = 64
SEQ = 197


EPS = 1e-06
SQRT_HALF = 0.7071067811865476
INV_ROOT_TWO_PI = 0.3989422804014327


def layer_norm(rows_in, norm_gain, norm_shift):
    average = jnp.mean(rows_in, axis=-1, keepdims=True)
    centred = rows_in - average
    inv_std = lax.rsqrt(jnp.mean(centred * centred, axis=-1, keepdims=True) + EPS)
    normed = centred * inv_std
    return (normed, inv_std, normed * norm_gain + norm_shift)


def norm_back(grad_rows, normed, inv_std, norm_gain):
    scaled = grad_rows * norm_gain
    inner = (
        scaled
        - jnp.mean(scaled, axis=-1, keepdims=True)
        - normed * jnp.mean(scaled * normed, axis=-1, keepdims=True)
    )
    return (inner * inv_std, jnp.sum(grad_rows * normed, axis=0), jnp.sum(grad_rows, axis=0))


def gelu_parts(pre_act):
    cumul = 0.5 * (1.0 + lax.erf(pre_act * SQRT_HALF))
    return (pre_act * cumul, cumul + pre_act * jnp.exp(-0.5 * pre_act * pre_act) * INV_ROOT_TWO_PI)


def route_table(expert_ids, slot_ids, experts, capacity):
    positions = jnp.arange(experts * capacity, dtype=jnp.int32)
    tables = []
    for choose in range(2):
        kept = slot_ids[:, choose] < capacity
        target = jnp.where(kept, expert_ids[:, choose] * capacity + slot_ids[:, choose], -1)
        tables.append((target[:, None] == positions[None, :]).astype(jnp.bfloat16))
    return tables


def pick_table(expert_ids, experts):
    labels = jnp.arange(experts, dtype=jnp.int32)
    return [
        (expert_ids[:, choose][:, None] == labels[None, :]).astype(jnp.float32)
        for choose in range(2)
    ]


def lane_pad(blocks):
    rows = blocks[0].shape[0]
    spare = -sum(block.shape[1] for block in blocks) % 128
    return jnp.concatenate(blocks + [jnp.zeros((rows, spare), blocks[0].dtype)], axis=1)


def other_replicas(value):
    size = lax.axis_size("replica")
    return [
        lax.ppermute(value, "replica", [(at, (at + step) % size) for at in range(size)])
        for step in range(1, size)
    ]


def to_expert(value, local_experts, capacity):
    shards, width = value.shape[0], value.shape[-1]
    return (
        value.reshape(shards, local_experts, capacity, width)
        .swapaxes(0, 1)
        .reshape(local_experts, shards * capacity, width)
    )


def from_expert(value, shards, capacity):
    local_experts, width = value.shape[0], value.shape[-1]
    return (
        value.reshape(local_experts, shards, capacity, width)
        .swapaxes(0, 1)
        .reshape(shards, local_experts * capacity, width)
    )


def expert_middle(rows, grad_rows, up_weight, up_bias, down_weight):
    expert_pre = (
        jnp.einsum("ecd,edf->ecf", rows, up_weight, preferred_element_type=jnp.float32)
        + up_bias.astype(jnp.float32)[:, None, :]
    )
    act_val, slope = gelu_parts(expert_pre)
    grad_active = jnp.einsum(
        "ecd,efd->ecf", grad_rows, down_weight, preferred_element_type=jnp.float32
    )
    return (act_val.astype(jnp.bfloat16), (grad_active * slope).astype(jnp.bfloat16))


def body(
    tokens,
    cotangent,
    norm1_gain,
    norm1_bias,
    proj_in,
    query_bias,
    value_bias,
    proj_out,
    out_bias,
    norm2_gain,
    norm2_bias,
    router,
    up_weight,
    up_bias,
    down_weight,
    down_bias,
    expert_ids,
    slot_ids,
):
    images = tokens.shape[0]
    small = jnp.stack(
        [norm1_gain, norm1_bias, query_bias, value_bias, out_bias, norm2_gain, norm2_bias],
        axis=1,
    )
    width_in, width_small = proj_in.shape[1], small.shape[1] + router.shape[1]
    first = lax.all_gather(
        lane_pad([proj_in, small, router]), "shard", axis=0, tiled=True
    )
    outproj_full = lax.all_gather(proj_out, "shard", axis=0, tiled=True)
    proj_full = first[:, :width_in]
    small_full = first[:, width_in : width_in + small.shape[1]]
    router_full = first[:, width_in + small.shape[1] : width_in + width_small]
    (
        gain_one,
        shift_one,
        query_shift,
        value_shift,
        out_shift,
        gain_two,
        shift_two,
    ) = [row for row in small_full.T]
    tok_rows = tokens.reshape(-1, D).astype(jnp.float32)
    normed_one, inv_one, pre_one = layer_norm(
        tok_rows, gain_one.astype(jnp.float32), shift_one.astype(jnp.float32)
    )
    act_one = pre_one.astype(jnp.bfloat16)
    mixed = jnp.dot(act_one, proj_full, preferred_element_type=jnp.float32)
    query_part = (mixed[:, :D] + query_shift.astype(jnp.float32)).astype(jnp.bfloat16)
    key_part = mixed[:, D : 2 * D].astype(jnp.bfloat16)
    value_part = (mixed[:, 2 * D :] + value_shift.astype(jnp.float32)).astype(jnp.bfloat16)
    query_heads = query_part.reshape(images, SEQ, HEADS, HDIM)
    key_heads = key_part.reshape(images, SEQ, HEADS, HDIM)
    value_heads = value_part.reshape(images, SEQ, HEADS, HDIM)
    scores = jnp.einsum(
        "ishd,ithd->ihst", query_heads, key_heads, preferred_element_type=jnp.float32
    ) * HDIM ** (-0.5)
    log_total = jnp.log(jnp.sum(jnp.exp(scores), axis=-1))
    attn_probs = jnp.exp(scores - log_total[..., None]).astype(jnp.bfloat16)
    context = (
        jnp.einsum("ihst,ithd->ishd", attn_probs, value_heads, preferred_element_type=jnp.float32)
        .reshape(-1, D)
        .astype(jnp.bfloat16)
    )
    resid = (
        tok_rows
        + jnp.dot(context, outproj_full, preferred_element_type=jnp.float32)
        + out_shift.astype(jnp.float32)
    )
    normed_two, inv_two, pre_two = layer_norm(
        resid, gain_two.astype(jnp.float32), shift_two.astype(jnp.float32)
    )
    hidden = pre_two.astype(jnp.bfloat16)
    logits = jnp.dot(hidden, router_full, preferred_element_type=jnp.float32)
    exp_logits = jnp.exp(logits)
    gate_probs = exp_logits / jnp.sum(exp_logits, axis=-1, keepdims=True)
    local_experts = up_weight.shape[0]
    experts = local_experts * lax.axis_size("shard")
    capacity = 2 * tok_rows.shape[0] // experts
    routes = route_table(expert_ids, slot_ids, experts, capacity)
    picks = pick_table(expert_ids, experts)
    both = jnp.concatenate(routes, axis=0)
    either = routes[0] + routes[1]
    gate_pair = [jnp.sum(gate_probs * pick, axis=-1) for pick in picks]
    grad_out = cotangent.reshape(-1, D).astype(jnp.float32)
    sent = jnp.concatenate(
        [(gate[:, None] * grad_out).astype(jnp.bfloat16) for gate in gate_pair], axis=0
    )
    buffer = jnp.dot(either.T, hidden, preferred_element_type=jnp.float32)
    grad_buffer = jnp.dot(both.T, sent, preferred_element_type=jnp.float32)
    shards = lax.axis_size("shard")
    outgoing = (
        jnp.concatenate([buffer, grad_buffer], axis=1)
        .astype(jnp.bfloat16)
        .reshape(shards, local_experts * capacity, 2 * D)
    )
    landed = to_expert(
        lax.all_to_all(outgoing, "shard", split_axis=0, concat_axis=0, tiled=True),
        local_experts,
        capacity,
    )
    arrived, grad_arrived = landed[..., :D], landed[..., D:]
    others = other_replicas(landed)
    active, grad_pre = expert_middle(arrived, grad_arrived, up_weight, up_bias, down_weight)
    expert_out = (
        jnp.einsum("ecf,efd->ecd", active, down_weight, preferred_element_type=jnp.float32)
        + down_bias.astype(jnp.float32)[:, None, :]
    ).astype(jnp.bfloat16)
    grad_in = jnp.einsum(
        "ecf,edf->ecd", grad_pre, up_weight, preferred_element_type=jnp.float32
    ).astype(jnp.bfloat16)
    answer = from_expert(jnp.concatenate([expert_out, grad_in], axis=2), shards, capacity)
    back = lax.all_to_all(answer, "shard", split_axis=0, concat_axis=0, tiled=True).reshape(
        experts * capacity, 2 * D
    )
    returned, grad_back = back[:, :D], back[:, D:]

    replicas = lax.axis_size("replica")
    ours = lax.axis_index("replica")
    part = up_weight.shape[2] // replicas
    up_part = lax.dynamic_slice_in_dim(up_weight, ours * part, part, axis=2)
    up_bias_part = lax.dynamic_slice_in_dim(up_bias, ours * part, part, axis=1)
    down_part = lax.dynamic_slice_in_dim(down_weight, ours * part, part, axis=1)
    active_parts = [lax.dynamic_slice_in_dim(active, ours * part, part, axis=2)]
    grad_pre_parts = [lax.dynamic_slice_in_dim(grad_pre, ours * part, part, axis=2)]
    for other in others:
        other_active, other_pre = expert_middle(
            other[..., :D], other[..., D:], up_part, up_bias_part, down_part
        )
        active_parts.append(other_active)
        grad_pre_parts.append(other_pre)
    all_rows = jnp.concatenate([landed] + others, axis=1)
    all_active = jnp.concatenate(active_parts, axis=1)
    all_pre = jnp.concatenate(grad_pre_parts, axis=1)
    width_part = D // replicas
    expert_grads = (
        jnp.einsum("ecd,ecf->edf", all_rows[..., :D], all_pre, preferred_element_type=jnp.float32),
        jnp.sum(all_pre, axis=1, dtype=jnp.float32),
        jnp.einsum(
            "ecf,ecd->efd", all_active, all_rows[..., D:], preferred_element_type=jnp.float32
        ),
        lax.dynamic_slice_in_dim(
            jnp.sum(all_rows[..., D:], axis=1, dtype=jnp.float32),
            ours * width_part,
            width_part,
            axis=1,
        ),
    )

    rows_here = tok_rows.shape[0]
    gathered_both = jnp.dot(both, returned, preferred_element_type=jnp.float32)
    gathered_pair = [gathered_both[:rows_here], gathered_both[rows_here:]]
    moe_sum = gate_pair[0][:, None] * gathered_pair[0] + gate_pair[1][:, None] * gathered_pair[1]
    block_out = (resid + moe_sum).astype(jnp.bfloat16).reshape(tokens.shape)
    grad_gate = [jnp.sum(grad_out * part_k, axis=-1) for part_k in gathered_pair]
    back_gain_one, back_proj, back_outproj, back_gain_two, back_router = (
        gain_one,
        proj_full,
        outproj_full,
        gain_two,
        router_full,
    )
    grad_moe = jnp.dot(either, grad_back, preferred_element_type=jnp.float32)
    grad_gates = picks[0] * grad_gate[0][:, None] + picks[1] * grad_gate[1][:, None]
    grad_logits = (
        gate_probs * (grad_gates - jnp.sum(gate_probs * grad_gates, axis=-1, keepdims=True))
    ).astype(jnp.bfloat16)
    router_term = jnp.dot(hidden.T, grad_logits, preferred_element_type=jnp.float32)
    grad_norm_two = grad_moe + jnp.dot(
        grad_logits, back_router.T, preferred_element_type=jnp.float32
    )
    grad_resid_two, gain_two_term, shift_two_term = norm_back(
        grad_norm_two, normed_two, inv_two, back_gain_two.astype(jnp.float32)
    )
    grad_resid = grad_out + grad_resid_two
    resid_bf = grad_resid.astype(jnp.bfloat16)
    out_shift_term = jnp.sum(grad_resid, axis=0)
    outproj_term = jnp.dot(context.T, resid_bf, preferred_element_type=jnp.float32)
    early = lax.psum_scatter(
        lane_pad(
            [
                outproj_term.astype(jnp.bfloat16),
                jnp.stack([out_shift_term, gain_two_term, shift_two_term], axis=0)
                .astype(jnp.bfloat16)
                .T,
                router_term.astype(jnp.bfloat16),
            ]
        ),
        "shard",
        scatter_dimension=0,
        tiled=True,
    )
    grad_context = (
        jnp.dot(resid_bf, back_outproj.T, preferred_element_type=jnp.float32)
        .astype(jnp.bfloat16)
        .reshape(images, SEQ, HEADS, HDIM)
    )
    scores_again = jnp.einsum(
        "ishd,ithd->ihst", query_heads, key_heads, preferred_element_type=jnp.float32
    ) * HDIM ** (-0.5)
    probs_full = jnp.exp(scores_again - log_total[..., None])
    grad_probs = jnp.einsum(
        "ishd,ithd->ihst", grad_context, value_heads, preferred_element_type=jnp.float32
    )
    grad_scores = (
        probs_full
        * (grad_probs - jnp.sum(probs_full * grad_probs, axis=-1, keepdims=True))
        * HDIM ** (-0.5)
    ).astype(jnp.bfloat16)
    probs_bf = probs_full.astype(jnp.bfloat16)
    grad_value = jnp.einsum(
        "ihst,ishd->ithd", probs_bf, grad_context, preferred_element_type=jnp.float32
    ).reshape(-1, D)
    grad_query = jnp.einsum(
        "ihst,ithd->ishd", grad_scores, key_heads, preferred_element_type=jnp.float32
    ).reshape(-1, D)
    grad_key = jnp.einsum(
        "ihst,ishd->ithd", grad_scores, query_heads, preferred_element_type=jnp.float32
    ).reshape(-1, D)
    grad_mixed = jnp.concatenate([grad_query, grad_key, grad_value], axis=1).astype(jnp.bfloat16)
    proj_term = jnp.dot(act_one.T, grad_mixed, preferred_element_type=jnp.float32)
    grad_act = jnp.dot(grad_mixed, back_proj.T, preferred_element_type=jnp.float32)
    grad_tok_norm, gain_one_term, shift_one_term = norm_back(
        grad_act, normed_one, inv_one, back_gain_one.astype(jnp.float32)
    )
    tokens_grad = (grad_resid + grad_tok_norm).astype(jnp.bfloat16).reshape(tokens.shape)
    query_shift_term = jnp.sum(grad_query, axis=0)
    value_shift_term = jnp.sum(grad_value, axis=0)
    late = lax.psum_scatter(
        lane_pad(
            [
                proj_term.astype(jnp.bfloat16),
                jnp.stack(
                    [gain_one_term, shift_one_term, query_shift_term, value_shift_term], axis=0
                )
                .astype(jnp.bfloat16)
                .T,
            ]
        ),
        "shard",
        scatter_dimension=0,
        tiled=True,
    )
    early_sum = early.astype(jnp.float32)
    for other in other_replicas(early):
        early_sum = early_sum + other.astype(jnp.float32)
    late_sum = late.astype(jnp.float32)
    for other in other_replicas(late):
        late_sum = late_sum + other.astype(jnp.float32)
    late_small = late_sum[:, width_in:]
    early_small = early_sum[:, D:]
    dense_grads = (
        late_small[:, 0],
        late_small[:, 1],
        late_sum[:, :width_in],
        late_small[:, 2],
        late_small[:, 3],
        early_sum[:, :D],
        early_small[:, 0],
        early_small[:, 1],
        early_small[:, 2],
        early_small[:, 3 : 3 + experts],
    )
    return (
        block_out,
        tokens_grad,
        dense_grads[0],
        dense_grads[1],
        dense_grads[2],
        dense_grads[3],
        dense_grads[4],
        dense_grads[5],
        dense_grads[6],
        dense_grads[7],
        dense_grads[8],
        dense_grads[9],
        expert_grads[0],
        expert_grads[1],
        expert_grads[2],
        expert_grads[3],
    )


def solution(mesh):
    in_specs = (
        P(("replica", "shard"), None, None),
        P(("replica", "shard"), None, None),
        P("shard"),
        P("shard"),
        P("shard", None),
        P("shard"),
        P("shard"),
        P("shard", None),
        P("shard"),
        P("shard"),
        P("shard"),
        P("shard", None),
        P("shard", None, None),
        P("shard", None),
        P("shard", None, None),
        P("shard", None),
        P(("replica", "shard"), None),
        P(("replica", "shard"), None),
    )
    out_specs = (
        P(("replica", "shard"), None, None),
        P(("replica", "shard"), None, None),
        P("shard"),
        P("shard"),
        P("shard", None),
        P("shard"),
        P("shard"),
        P("shard", None),
        P("shard"),
        P("shard"),
        P("shard"),
        P("shard", None),
        P("shard", None, "replica"),
        P("shard", "replica"),
        P("shard", "replica", None),
        P("shard", "replica"),
    )
    return jax.shard_map(body, mesh=mesh, in_specs=in_specs, out_specs=out_specs, check_vma=False)
```

```python
import jax
import jax.numpy as jnp
from jax import lax
from jax.sharding import PartitionSpec as P

D = 768
HEADS = 12
HDIM = 64
SEQ = 197


EPS = 1e-06
SQRT_HALF = 0.7071067811865476
INV_ROOT_TWO_PI = 0.3989422804014327


def layer_norm(rows_in, norm_gain, norm_shift):
    average = jnp.mean(rows_in, axis=-1, keepdims=True)
    centred = rows_in - average
    inv_std = lax.rsqrt(jnp.mean(centred * centred, axis=-1, keepdims=True) + EPS)
    normed = centred * inv_std
    return (normed, inv_std, normed * norm_gain + norm_shift)


def norm_back(grad_rows, normed, inv_std, norm_gain):
    scaled = grad_rows * norm_gain
    inner = (
        scaled
        - jnp.mean(scaled, axis=-1, keepdims=True)
        - normed * jnp.mean(scaled * normed, axis=-1, keepdims=True)
    )
    return (inner * inv_std, jnp.sum(grad_rows * normed, axis=0), jnp.sum(grad_rows, axis=0))


def gelu_parts(pre_act):
    cumul = 0.5 * (1.0 + lax.erf(pre_act * SQRT_HALF))
    return (pre_act * cumul, cumul + pre_act * jnp.exp(-0.5 * pre_act * pre_act) * INV_ROOT_TWO_PI)


def route_table(expert_ids, slot_ids, experts, capacity):
    positions = jnp.arange(experts * capacity, dtype=jnp.int32)
    tables = []
    for choose in range(2):
        kept = slot_ids[:, choose] < capacity
        target = jnp.where(kept, expert_ids[:, choose] * capacity + slot_ids[:, choose], -1)
        tables.append((target[:, None] == positions[None, :]).astype(jnp.bfloat16))
    return tables


def pick_table(expert_ids, experts):
    labels = jnp.arange(experts, dtype=jnp.int32)
    return [
        (expert_ids[:, choose][:, None] == labels[None, :]).astype(jnp.float32)
        for choose in range(2)
    ]


def lane_pad(blocks):
    rows = blocks[0].shape[0]
    spare = -sum(block.shape[1] for block in blocks) % 128
    return jnp.concatenate(blocks + [jnp.zeros((rows, spare), blocks[0].dtype)], axis=1)


def other_replicas(value):
    size = lax.axis_size("replica")
    return [
        lax.ppermute(value, "replica", [(at, (at + step) % size) for at in range(size)])
        for step in range(1, size)
    ]


def to_expert(value, local_experts, capacity):
    shards, width = value.shape[0], value.shape[-1]
    return (
        value.reshape(shards, local_experts, capacity, width)
        .swapaxes(0, 1)
        .reshape(local_experts, shards * capacity, width)
    )


def from_expert(value, shards, capacity):
    local_experts, width = value.shape[0], value.shape[-1]
    return (
        value.reshape(local_experts, shards, capacity, width)
        .swapaxes(0, 1)
        .reshape(shards, local_experts * capacity, width)
    )


def expert_middle(rows, grad_rows, up_weight, up_bias, down_weight):
    expert_pre = (
        jnp.einsum("ecd,edf->ecf", rows, up_weight, preferred_element_type=jnp.float32)
        + up_bias.astype(jnp.float32)[:, None, :]
    )
    act_val, slope = gelu_parts(expert_pre)
    grad_active = jnp.einsum(
        "ecd,efd->ecf", grad_rows, down_weight, preferred_element_type=jnp.float32
    )
    return (act_val.astype(jnp.bfloat16), (grad_active * slope).astype(jnp.bfloat16))


def body(
    tokens,
    cotangent,
    norm1_gain,
    norm1_bias,
    proj_in,
    query_bias,
    value_bias,
    proj_out,
    out_bias,
    norm2_gain,
    norm2_bias,
    router,
    up_weight,
    up_bias,
    down_weight,
    down_bias,
    expert_ids,
    slot_ids,
):
    images = tokens.shape[0]
    small = jnp.stack(
        [norm1_gain, norm1_bias, query_bias, value_bias, out_bias, norm2_gain, norm2_bias],
        axis=1,
    )
    width_in, width_small = proj_in.shape[1], small.shape[1] + router.shape[1]
    first = lax.all_gather(
        lane_pad([proj_in, proj_out, small, router]), "shard", axis=0, tiled=True
    )
    width_both = width_in + proj_out.shape[1]
    proj_full = first[:, :width_in]
    outproj_full = first[:, width_in:width_both]
    small_full = first[:, width_both : width_both + small.shape[1]]
    router_full = first[:, width_both + small.shape[1] : width_both + width_small]
    (
        gain_one,
        shift_one,
        query_shift,
        value_shift,
        out_shift,
        gain_two,
        shift_two,
    ) = [row for row in small_full.T]
    tok_rows = tokens.reshape(-1, D).astype(jnp.float32)
    normed_one, inv_one, pre_one = layer_norm(
        tok_rows, gain_one.astype(jnp.float32), shift_one.astype(jnp.float32)
    )
    act_one = pre_one.astype(jnp.bfloat16)
    mixed = jnp.dot(act_one, proj_full, preferred_element_type=jnp.float32)
    query_part = (mixed[:, :D] + query_shift.astype(jnp.float32)).astype(jnp.bfloat16)
    key_part = mixed[:, D : 2 * D].astype(jnp.bfloat16)
    value_part = (mixed[:, 2 * D :] + value_shift.astype(jnp.float32)).astype(jnp.bfloat16)
    query_heads = query_part.reshape(images, SEQ, HEADS, HDIM)
    key_heads = key_part.reshape(images, SEQ, HEADS, HDIM)
    value_heads = value_part.reshape(images, SEQ, HEADS, HDIM)
    scores = jnp.einsum(
        "ishd,ithd->ihst", query_heads, key_heads, preferred_element_type=jnp.float32
    ) * HDIM ** (-0.5)
    log_total = jnp.log(jnp.sum(jnp.exp(scores), axis=-1))
    attn_probs = jnp.exp(scores - log_total[..., None]).astype(jnp.bfloat16)
    context = (
        jnp.einsum("ihst,ithd->ishd", attn_probs, value_heads, preferred_element_type=jnp.float32)
        .reshape(-1, D)
        .astype(jnp.bfloat16)
    )
    resid = (
        tok_rows
        + jnp.dot(context, outproj_full, preferred_element_type=jnp.float32)
        + out_shift.astype(jnp.float32)
    )
    normed_two, inv_two, pre_two = layer_norm(
        resid, gain_two.astype(jnp.float32), shift_two.astype(jnp.float32)
    )
    hidden = pre_two.astype(jnp.bfloat16)
    logits = jnp.dot(hidden, router_full, preferred_element_type=jnp.float32)
    exp_logits = jnp.exp(logits)
    gate_probs = exp_logits / jnp.sum(exp_logits, axis=-1, keepdims=True)
    local_experts = up_weight.shape[0]
    experts = local_experts * lax.axis_size("shard")
    capacity = 2 * tok_rows.shape[0] // experts
    routes = route_table(expert_ids, slot_ids, experts, capacity)
    picks = pick_table(expert_ids, experts)
    both = jnp.concatenate(routes, axis=0)
    either = routes[0] + routes[1]
    gate_pair = [jnp.sum(gate_probs * pick, axis=-1) for pick in picks]
    grad_out = cotangent.reshape(-1, D).astype(jnp.float32)
    sent = jnp.concatenate(
        [(gate[:, None] * grad_out).astype(jnp.bfloat16) for gate in gate_pair], axis=0
    )
    buffer = jnp.dot(either.T, hidden, preferred_element_type=jnp.float32)
    grad_buffer = jnp.dot(both.T, sent, preferred_element_type=jnp.float32)
    shards = lax.axis_size("shard")
    outgoing = (
        jnp.concatenate([buffer, grad_buffer], axis=1)
        .astype(jnp.bfloat16)
        .reshape(shards, local_experts * capacity, 2 * D)
    )
    landed = to_expert(
        lax.all_to_all(outgoing, "shard", split_axis=0, concat_axis=0, tiled=True),
        local_experts,
        capacity,
    )
    arrived, grad_arrived = landed[..., :D], landed[..., D:]
    others = other_replicas(landed)
    active, grad_pre = expert_middle(arrived, grad_arrived, up_weight, up_bias, down_weight)
    expert_out = (
        jnp.einsum("ecf,efd->ecd", active, down_weight, preferred_element_type=jnp.float32)
        + down_bias.astype(jnp.float32)[:, None, :]
    ).astype(jnp.bfloat16)
    grad_in = jnp.einsum(
        "ecf,edf->ecd", grad_pre, up_weight, preferred_element_type=jnp.float32
    ).astype(jnp.bfloat16)
    answer = from_expert(jnp.concatenate([expert_out, grad_in], axis=2), shards, capacity)
    back = lax.all_to_all(answer, "shard", split_axis=0, concat_axis=0, tiled=True).reshape(
        experts * capacity, 2 * D
    )
    returned, grad_back = back[:, :D], back[:, D:]

    replicas = lax.axis_size("replica")
    ours = lax.axis_index("replica")
    part = up_weight.shape[2] // replicas
    up_part = lax.dynamic_slice_in_dim(up_weight, ours * part, part, axis=2)
    up_bias_part = lax.dynamic_slice_in_dim(up_bias, ours * part, part, axis=1)
    down_part = lax.dynamic_slice_in_dim(down_weight, ours * part, part, axis=1)
    active_parts = [lax.dynamic_slice_in_dim(active, ours * part, part, axis=2)]
    grad_pre_parts = [lax.dynamic_slice_in_dim(grad_pre, ours * part, part, axis=2)]
    for other in others:
        other_active, other_pre = expert_middle(
            other[..., :D], other[..., D:], up_part, up_bias_part, down_part
        )
        active_parts.append(other_active)
        grad_pre_parts.append(other_pre)
    all_rows = jnp.concatenate([landed] + others, axis=1)
    all_active = jnp.concatenate(active_parts, axis=1)
    all_pre = jnp.concatenate(grad_pre_parts, axis=1)
    width_part = D // replicas
    expert_grads = (
        jnp.einsum("ecd,ecf->edf", all_rows[..., :D], all_pre, preferred_element_type=jnp.float32),
        jnp.sum(all_pre, axis=1, dtype=jnp.float32),
        jnp.einsum(
            "ecf,ecd->efd", all_active, all_rows[..., D:], preferred_element_type=jnp.float32
        ),
        lax.dynamic_slice_in_dim(
            jnp.sum(all_rows[..., D:], axis=1, dtype=jnp.float32),
            ours * width_part,
            width_part,
            axis=1,
        ),
    )

    rows_here = tok_rows.shape[0]
    gathered_both = jnp.dot(both, returned, preferred_element_type=jnp.float32)
    gathered_pair = [gathered_both[:rows_here], gathered_both[rows_here:]]
    moe_sum = gate_pair[0][:, None] * gathered_pair[0] + gate_pair[1][:, None] * gathered_pair[1]
    block_out = (resid + moe_sum).astype(jnp.bfloat16).reshape(tokens.shape)
    grad_gate = [jnp.sum(grad_out * part_k, axis=-1) for part_k in gathered_pair]
    back_gain_one, back_proj, back_outproj, back_gain_two, back_router = (
        gain_one,
        proj_full,
        outproj_full,
        gain_two,
        router_full,
    )
    grad_moe = jnp.dot(either, grad_back, preferred_element_type=jnp.float32)
    grad_gates = picks[0] * grad_gate[0][:, None] + picks[1] * grad_gate[1][:, None]
    grad_logits = (
        gate_probs * (grad_gates - jnp.sum(gate_probs * grad_gates, axis=-1, keepdims=True))
    ).astype(jnp.bfloat16)
    router_term = jnp.dot(hidden.T, grad_logits, preferred_element_type=jnp.float32)
    grad_norm_two = grad_moe + jnp.dot(
        grad_logits, back_router.T, preferred_element_type=jnp.float32
    )
    grad_resid_two, gain_two_term, shift_two_term = norm_back(
        grad_norm_two, normed_two, inv_two, back_gain_two.astype(jnp.float32)
    )
    grad_resid = grad_out + grad_resid_two
    resid_bf = grad_resid.astype(jnp.bfloat16)
    out_shift_term = jnp.sum(grad_resid, axis=0)
    outproj_term = jnp.dot(context.T, resid_bf, preferred_element_type=jnp.float32)
    grad_context = (
        jnp.dot(resid_bf, back_outproj.T, preferred_element_type=jnp.float32)
        .astype(jnp.bfloat16)
        .reshape(images, SEQ, HEADS, HDIM)
    )
    scores_again = jnp.einsum(
        "ishd,ithd->ihst", query_heads, key_heads, preferred_element_type=jnp.float32
    ) * HDIM ** (-0.5)
    probs_full = jnp.exp(scores_again - log_total[..., None])
    grad_probs = jnp.einsum(
        "ishd,ithd->ihst", grad_context, value_heads, preferred_element_type=jnp.float32
    )
    grad_scores = (
        probs_full
        * (grad_probs - jnp.sum(probs_full * grad_probs, axis=-1, keepdims=True))
        * HDIM ** (-0.5)
    ).astype(jnp.bfloat16)
    probs_bf = probs_full.astype(jnp.bfloat16)
    grad_value = jnp.einsum(
        "ihst,ishd->ithd", probs_bf, grad_context, preferred_element_type=jnp.float32
    ).reshape(-1, D)
    grad_query = jnp.einsum(
        "ihst,ithd->ishd", grad_scores, key_heads, preferred_element_type=jnp.float32
    ).reshape(-1, D)
    grad_key = jnp.einsum(
        "ihst,ishd->ithd", grad_scores, query_heads, preferred_element_type=jnp.float32
    ).reshape(-1, D)
    grad_mixed = jnp.concatenate([grad_query, grad_key, grad_value], axis=1).astype(jnp.bfloat16)
    proj_term = jnp.dot(act_one.T, grad_mixed, preferred_element_type=jnp.float32)
    grad_act = jnp.dot(grad_mixed, back_proj.T, preferred_element_type=jnp.float32)
    grad_tok_norm, gain_one_term, shift_one_term = norm_back(
        grad_act, normed_one, inv_one, back_gain_one.astype(jnp.float32)
    )
    tokens_grad = (grad_resid + grad_tok_norm).astype(jnp.bfloat16).reshape(tokens.shape)
    query_shift_term = jnp.sum(grad_query, axis=0)
    value_shift_term = jnp.sum(grad_value, axis=0)
    column_sums = [
        gain_one_term,
        shift_one_term,
        query_shift_term,
        value_shift_term,
        out_shift_term,
        gain_two_term,
        shift_two_term,
    ]
    summed = lax.psum_scatter(
        lane_pad(
            [
                proj_term.astype(jnp.bfloat16),
                outproj_term.astype(jnp.bfloat16),
                jnp.stack(column_sums, axis=0).astype(jnp.bfloat16).T,
                router_term.astype(jnp.bfloat16),
            ]
        ),
        "shard",
        scatter_dimension=0,
        tiled=True,
    )
    total = summed.astype(jnp.float32)
    for other in other_replicas(summed):
        total = total + other.astype(jnp.float32)
    small_total = total[:, width_both:]
    columns = len(column_sums)
    dense_grads = (
        small_total[:, 0],
        small_total[:, 1],
        total[:, :width_in],
        small_total[:, 2],
        small_total[:, 3],
        total[:, width_in:width_both],
        small_total[:, 4],
        small_total[:, 5],
        small_total[:, 6],
        small_total[:, columns : columns + experts],
    )
    return (
        block_out,
        tokens_grad,
        dense_grads[0],
        dense_grads[1],
        dense_grads[2],
        dense_grads[3],
        dense_grads[4],
        dense_grads[5],
        dense_grads[6],
        dense_grads[7],
        dense_grads[8],
        dense_grads[9],
        expert_grads[0],
        expert_grads[1],
        expert_grads[2],
        expert_grads[3],
    )


def solution(mesh):
    in_specs = (
        P(("replica", "shard"), None, None),
        P(("replica", "shard"), None, None),
        P("shard"),
        P("shard"),
        P("shard", None),
        P("shard"),
        P("shard"),
        P("shard", None),
        P("shard"),
        P("shard"),
        P("shard"),
        P("shard", None),
        P("shard", None, None),
        P("shard", None),
        P("shard", None, None),
        P("shard", None),
        P(("replica", "shard"), None),
        P(("replica", "shard"), None),
    )
    out_specs = (
        P(("replica", "shard"), None, None),
        P(("replica", "shard"), None, None),
        P("shard"),
        P("shard"),
        P("shard", None),
        P("shard"),
        P("shard"),
        P("shard", None),
        P("shard"),
        P("shard"),
        P("shard"),
        P("shard", None),
        P("shard", None, "replica"),
        P("shard", "replica"),
        P("shard", "replica", None),
        P("shard", "replica"),
    )
    return jax.shard_map(body, mesh=mesh, in_specs=in_specs, out_specs=out_specs, check_vma=False)
```

```python
import jax
import jax.numpy as jnp
from jax import lax
from jax.sharding import PartitionSpec as P

D = 768
HEADS = 12
HDIM = 64
SEQ = 197


EPS = 1e-06
SQRT_HALF = 0.7071067811865476
INV_ROOT_TWO_PI = 0.3989422804014327


def layer_norm(rows_in, norm_gain, norm_shift):
    average = jnp.mean(rows_in, axis=-1, keepdims=True)
    centred = rows_in - average
    inv_std = lax.rsqrt(jnp.mean(centred * centred, axis=-1, keepdims=True) + EPS)
    normed = centred * inv_std
    return (normed, inv_std, normed * norm_gain + norm_shift)


def norm_back(grad_rows, normed, inv_std, norm_gain):
    scaled = grad_rows * norm_gain
    inner = (
        scaled
        - jnp.mean(scaled, axis=-1, keepdims=True)
        - normed * jnp.mean(scaled * normed, axis=-1, keepdims=True)
    )
    return (inner * inv_std, jnp.sum(grad_rows * normed, axis=0), jnp.sum(grad_rows, axis=0))


def gelu_parts(pre_act):
    cumul = 0.5 * (1.0 + lax.erf(pre_act * SQRT_HALF))
    return (pre_act * cumul, cumul + pre_act * jnp.exp(-0.5 * pre_act * pre_act) * INV_ROOT_TWO_PI)


def route_table(expert_ids, slot_ids, experts, capacity):
    positions = jnp.arange(experts * capacity, dtype=jnp.int32)
    tables = []
    for choose in range(2):
        kept = slot_ids[:, choose] < capacity
        target = jnp.where(kept, expert_ids[:, choose] * capacity + slot_ids[:, choose], -1)
        tables.append((target[:, None] == positions[None, :]).astype(jnp.bfloat16))
    return tables


def pick_table(expert_ids, experts):
    labels = jnp.arange(experts, dtype=jnp.int32)
    return [
        (expert_ids[:, choose][:, None] == labels[None, :]).astype(jnp.float32)
        for choose in range(2)
    ]


def lane_pad(blocks):
    rows = blocks[0].shape[0]
    spare = -sum(block.shape[1] for block in blocks) % 128
    return jnp.concatenate(blocks + [jnp.zeros((rows, spare), blocks[0].dtype)], axis=1)


def other_replicas(value):
    size = lax.axis_size("replica")
    return [
        lax.ppermute(value, "replica", [(at, (at + step) % size) for at in range(size)])
        for step in range(1, size)
    ]


def to_expert(value, local_experts, capacity):
    shards, width = value.shape[0], value.shape[-1]
    return (
        value.reshape(shards, local_experts, capacity, width)
        .swapaxes(0, 1)
        .reshape(local_experts, shards * capacity, width)
    )


def from_expert(value, shards, capacity):
    local_experts, width = value.shape[0], value.shape[-1]
    return (
        value.reshape(local_experts, shards, capacity, width)
        .swapaxes(0, 1)
        .reshape(shards, local_experts * capacity, width)
    )


def expert_middle(rows, grad_rows, up_weight, up_bias, down_weight):
    expert_pre = (
        jnp.einsum("ecd,edf->ecf", rows, up_weight, preferred_element_type=jnp.float32)
        + up_bias.astype(jnp.float32)[:, None, :]
    )
    act_val, slope = gelu_parts(expert_pre)
    grad_active = jnp.einsum(
        "ecd,efd->ecf", grad_rows, down_weight, preferred_element_type=jnp.float32
    )
    return (act_val.astype(jnp.bfloat16), (grad_active * slope).astype(jnp.bfloat16))


def body(
    tokens,
    cotangent,
    norm1_gain,
    norm1_bias,
    proj_in,
    query_bias,
    value_bias,
    proj_out,
    out_bias,
    norm2_gain,
    norm2_bias,
    router,
    up_weight,
    up_bias,
    down_weight,
    down_bias,
    expert_ids,
    slot_ids,
):
    images = tokens.shape[0]
    small = jnp.stack(
        [norm1_gain, norm1_bias, query_bias, value_bias, out_bias, norm2_gain, norm2_bias],
        axis=1,
    )
    width_in, width_small = proj_in.shape[1], small.shape[1] + router.shape[1]
    first = lax.all_gather(
        lane_pad([proj_in, proj_out, small, router]), "shard", axis=0, tiled=True
    )
    width_both = width_in + proj_out.shape[1]
    proj_full = first[:, :width_in]
    outproj_full = first[:, width_in:width_both]
    small_full = first[:, width_both : width_both + small.shape[1]]
    router_full = first[:, width_both + small.shape[1] : width_both + width_small]
    (
        gain_one,
        shift_one,
        query_shift,
        value_shift,
        out_shift,
        gain_two,
        shift_two,
    ) = [row for row in small_full.T]
    tok_rows = tokens.reshape(-1, D).astype(jnp.float32)
    normed_one, inv_one, pre_one = layer_norm(
        tok_rows, gain_one.astype(jnp.float32), shift_one.astype(jnp.float32)
    )
    act_one = pre_one.astype(jnp.bfloat16)
    mixed = jnp.dot(act_one, proj_full, preferred_element_type=jnp.float32)
    query_part = (mixed[:, :D] + query_shift.astype(jnp.float32)).astype(jnp.bfloat16)
    key_part = mixed[:, D : 2 * D].astype(jnp.bfloat16)
    value_part = (mixed[:, 2 * D :] + value_shift.astype(jnp.float32)).astype(jnp.bfloat16)
    query_heads = query_part.reshape(images, SEQ, HEADS, HDIM)
    key_heads = key_part.reshape(images, SEQ, HEADS, HDIM)
    value_heads = value_part.reshape(images, SEQ, HEADS, HDIM)
    scores = jnp.einsum(
        "ishd,ithd->ihst", query_heads, key_heads, preferred_element_type=jnp.float32
    ) * HDIM ** (-0.5)
    log_total = jnp.log(jnp.sum(jnp.exp(scores), axis=-1))
    attn_probs = jnp.exp(scores - log_total[..., None]).astype(jnp.bfloat16)
    context = (
        jnp.einsum("ihst,ithd->ishd", attn_probs, value_heads, preferred_element_type=jnp.float32)
        .reshape(-1, D)
        .astype(jnp.bfloat16)
    )
    resid = (
        tok_rows
        + jnp.dot(context, outproj_full, preferred_element_type=jnp.float32)
        + out_shift.astype(jnp.float32)
    )
    normed_two, inv_two, pre_two = layer_norm(
        resid, gain_two.astype(jnp.float32), shift_two.astype(jnp.float32)
    )
    hidden = pre_two.astype(jnp.bfloat16)
    logits = jnp.dot(hidden, router_full, preferred_element_type=jnp.float32)
    exp_logits = jnp.exp(logits)
    gate_probs = exp_logits / jnp.sum(exp_logits, axis=-1, keepdims=True)
    local_experts = up_weight.shape[0]
    experts = local_experts * lax.axis_size("shard")
    capacity = 2 * tok_rows.shape[0] // experts
    routes = route_table(expert_ids, slot_ids, experts, capacity)
    picks = pick_table(expert_ids, experts)
    both = jnp.concatenate(routes, axis=0)
    either = routes[0] + routes[1]
    gate_pair = [jnp.sum(gate_probs * pick, axis=-1) for pick in picks]
    grad_out = cotangent.reshape(-1, D).astype(jnp.float32)
    sent = jnp.concatenate(
        [(gate[:, None] * grad_out).astype(jnp.bfloat16) for gate in gate_pair], axis=0
    )
    buffer = jnp.dot(either.T, hidden, preferred_element_type=jnp.float32)
    grad_buffer = jnp.dot(both.T, sent, preferred_element_type=jnp.float32)
    shards = lax.axis_size("shard")
    outgoing = (
        jnp.concatenate([buffer, grad_buffer], axis=1)
        .astype(jnp.bfloat16)
        .reshape(shards, local_experts * capacity, 2 * D)
    )
    landed = to_expert(
        lax.all_to_all(outgoing, "shard", split_axis=0, concat_axis=0, tiled=True),
        local_experts,
        capacity,
    )
    arrived, grad_arrived = landed[..., :D], landed[..., D:]
    others = other_replicas(landed)
    active, grad_pre = expert_middle(arrived, grad_arrived, up_weight, up_bias, down_weight)
    expert_out = (
        jnp.einsum("ecf,efd->ecd", active, down_weight, preferred_element_type=jnp.float32)
        + down_bias.astype(jnp.float32)[:, None, :]
    ).astype(jnp.bfloat16)
    grad_in = jnp.einsum(
        "ecf,edf->ecd", grad_pre, up_weight, preferred_element_type=jnp.float32
    ).astype(jnp.bfloat16)
    answer = from_expert(jnp.concatenate([expert_out, grad_in], axis=2), shards, capacity)
    back = lax.all_to_all(answer, "shard", split_axis=0, concat_axis=0, tiled=True).reshape(
        experts * capacity, 2 * D
    )
    returned, grad_back = back[:, :D], back[:, D:]

    replicas = lax.axis_size("replica")
    ours = lax.axis_index("replica")
    part = up_weight.shape[2] // replicas
    up_part = lax.dynamic_slice_in_dim(up_weight, ours * part, part, axis=2)
    up_bias_part = lax.dynamic_slice_in_dim(up_bias, ours * part, part, axis=1)
    down_part = lax.dynamic_slice_in_dim(down_weight, ours * part, part, axis=1)
    active_parts = [lax.dynamic_slice_in_dim(active, ours * part, part, axis=2)]
    grad_pre_parts = [lax.dynamic_slice_in_dim(grad_pre, ours * part, part, axis=2)]
    for other in others:
        other_active, other_pre = expert_middle(
            other[..., :D], other[..., D:], up_part, up_bias_part, down_part
        )
        active_parts.append(other_active)
        grad_pre_parts.append(other_pre)
    all_rows = jnp.concatenate([landed] + others, axis=1)
    all_active = jnp.concatenate(active_parts, axis=1)
    all_pre = jnp.concatenate(grad_pre_parts, axis=1)
    width_part = D // replicas
    expert_grads = (
        jnp.einsum("ecd,ecf->edf", all_rows[..., :D], all_pre, preferred_element_type=jnp.float32),
        jnp.sum(all_pre, axis=1, dtype=jnp.float32),
        jnp.einsum(
            "ecf,ecd->efd", all_active, all_rows[..., D:], preferred_element_type=jnp.float32
        ),
        lax.dynamic_slice_in_dim(
            jnp.sum(all_rows[..., D:], axis=1, dtype=jnp.float32),
            ours * width_part,
            width_part,
            axis=1,
        ),
    )

    rows_here = tok_rows.shape[0]
    gathered_both = jnp.dot(both, returned, preferred_element_type=jnp.float32)
    gathered_pair = [gathered_both[:rows_here], gathered_both[rows_here:]]
    moe_sum = gate_pair[0][:, None] * gathered_pair[0] + gate_pair[1][:, None] * gathered_pair[1]
    block_out = (resid + moe_sum).astype(jnp.bfloat16).reshape(tokens.shape)
    grad_gate = [jnp.sum(grad_out * part_k, axis=-1) for part_k in gathered_pair]
    back_gain_one, back_proj, back_outproj, back_gain_two, back_router = (
        gain_one,
        proj_full,
        outproj_full,
        gain_two,
        router_full,
    )
    grad_moe = jnp.dot(either, grad_back, preferred_element_type=jnp.float32)
    grad_gates = picks[0] * grad_gate[0][:, None] + picks[1] * grad_gate[1][:, None]
    grad_logits = (
        gate_probs * (grad_gates - jnp.sum(gate_probs * grad_gates, axis=-1, keepdims=True))
    ).astype(jnp.bfloat16)
    router_term = jnp.dot(hidden.T, grad_logits, preferred_element_type=jnp.float32)
    grad_norm_two = grad_moe + jnp.dot(
        grad_logits, back_router.T, preferred_element_type=jnp.float32
    )
    grad_resid_two, gain_two_term, shift_two_term = norm_back(
        grad_norm_two, normed_two, inv_two, back_gain_two.astype(jnp.float32)
    )
    grad_resid = grad_out + grad_resid_two
    resid_bf = grad_resid.astype(jnp.bfloat16)
    out_shift_term = jnp.sum(grad_resid, axis=0)
    outproj_term = jnp.dot(context.T, resid_bf, preferred_element_type=jnp.float32)
    grad_context = (
        jnp.dot(resid_bf, back_outproj.T, preferred_element_type=jnp.float32)
        .astype(jnp.bfloat16)
        .reshape(images, SEQ, HEADS, HDIM)
    )
    scores_again = jnp.einsum(
        "ishd,ithd->ihst", query_heads, key_heads, preferred_element_type=jnp.float32
    ) * HDIM ** (-0.5)
    probs_full = jnp.exp(scores_again - log_total[..., None])
    grad_probs = jnp.einsum(
        "ishd,ithd->ihst", grad_context, value_heads, preferred_element_type=jnp.float32
    )
    grad_scores = (
        probs_full
        * (grad_probs - jnp.sum(probs_full * grad_probs, axis=-1, keepdims=True))
        * HDIM ** (-0.5)
    ).astype(jnp.bfloat16)
    probs_bf = probs_full.astype(jnp.bfloat16)
    grad_value = jnp.einsum(
        "ihst,ishd->ithd", probs_bf, grad_context, preferred_element_type=jnp.float32
    ).reshape(-1, D)
    grad_query = jnp.einsum(
        "ihst,ithd->ishd", grad_scores, key_heads, preferred_element_type=jnp.float32
    ).reshape(-1, D)
    grad_key = jnp.einsum(
        "ihst,ishd->ithd", grad_scores, query_heads, preferred_element_type=jnp.float32
    ).reshape(-1, D)
    grad_mixed = jnp.concatenate([grad_query, grad_key, grad_value], axis=1).astype(jnp.bfloat16)
    proj_term = jnp.dot(act_one.T, grad_mixed, preferred_element_type=jnp.float32)
    grad_act = jnp.dot(grad_mixed, back_proj.T, preferred_element_type=jnp.float32)
    grad_tok_norm, gain_one_term, shift_one_term = norm_back(
        grad_act, normed_one, inv_one, back_gain_one.astype(jnp.float32)
    )
    tokens_grad = (grad_resid + grad_tok_norm).astype(jnp.bfloat16).reshape(tokens.shape)
    query_shift_term = jnp.sum(grad_query, axis=0)
    value_shift_term = jnp.sum(grad_value, axis=0)
    column_sums = [
        gain_one_term,
        shift_one_term,
        query_shift_term,
        value_shift_term,
        out_shift_term,
        gain_two_term,
        shift_two_term,
    ]
    summed = lax.psum_scatter(
        lane_pad(
            [
                proj_term.astype(jnp.bfloat16),
                outproj_term.astype(jnp.bfloat16),
                lax.optimization_barrier(
                    lane_pad(
                        [
                            jnp.stack(column_sums, axis=0).astype(jnp.bfloat16).T,
                            router_term.astype(jnp.bfloat16),
                        ]
                    )
                ),
            ]
        ),
        "shard",
        scatter_dimension=0,
        tiled=True,
    )
    total = summed.astype(jnp.float32)
    for other in other_replicas(summed):
        total = total + other.astype(jnp.float32)
    small_total = total[:, width_both:]
    columns = len(column_sums)
    dense_grads = (
        small_total[:, 0],
        small_total[:, 1],
        total[:, :width_in],
        small_total[:, 2],
        small_total[:, 3],
        total[:, width_in:width_both],
        small_total[:, 4],
        small_total[:, 5],
        small_total[:, 6],
        small_total[:, columns : columns + experts],
    )
    return (
        block_out,
        tokens_grad,
        dense_grads[0],
        dense_grads[1],
        dense_grads[2],
        dense_grads[3],
        dense_grads[4],
        dense_grads[5],
        dense_grads[6],
        dense_grads[7],
        dense_grads[8],
        dense_grads[9],
        expert_grads[0],
        expert_grads[1],
        expert_grads[2],
        expert_grads[3],
    )


def solution(mesh):
    in_specs = (
        P(("replica", "shard"), None, None),
        P(("replica", "shard"), None, None),
        P("shard"),
        P("shard"),
        P("shard", None),
        P("shard"),
        P("shard"),
        P("shard", None),
        P("shard"),
        P("shard"),
        P("shard"),
        P("shard", None),
        P("shard", None, None),
        P("shard", None),
        P("shard", None, None),
        P("shard", None),
        P(("replica", "shard"), None),
        P(("replica", "shard"), None),
    )
    out_specs = (
        P(("replica", "shard"), None, None),
        P(("replica", "shard"), None, None),
        P("shard"),
        P("shard"),
        P("shard", None),
        P("shard"),
        P("shard"),
        P("shard", None),
        P("shard"),
        P("shard"),
        P("shard"),
        P("shard", None),
        P("shard", None, "replica"),
        P("shard", "replica"),
        P("shard", "replica", None),
        P("shard", "replica"),
    )
    return jax.shard_map(body, mesh=mesh, in_specs=in_specs, out_specs=out_specs, check_vma=False)
```
